256 devices in a mesh: grp: 4 (over z_lo, core), fsdp: 64 (over z_hi, x, y).
Axes of the slice: x: 4, y: 4, z: 8 (z_hi: 4, z_lo: 2; z = z_hi * 2 + z_lo), core: 2. Of those that a mesh axis runs over, the one named last changes fastest.
Arguments:
- layer_input_rows: bfloat16 [131072, 8192], P(('grp', 'fsdp')), may hold values from -400 to 400, as said below
- input_norm_gain: bfloat16 [8192], replicated, may hold values from 0.5 to 1.5
- key_value_codes: int32 [8192, 256], P('fsdp'), may hold values from 0 to 65535
- block_scale_codes: int32 [256, 128], P('fsdp'), may hold values from -2147483648 to 2147483646
- outer_scale_codes: int32 [512], P('fsdp'), may hold values from 0 to 255
- adapter_down_factor: bfloat16 [8192, 64], replicated, may hold values from -0.0625 to 0.0625
- adapter_up_factor: bfloat16 [64, 1024], replicated, may hold values from -0.75 to 0.75
- target: bfloat16 [131072, 1024], P(('grp', 'fsdp')), may hold values from -18 to 18
Outputs:
- kv: bfloat16 [131072, 1024], P(('grp', 'fsdp'))
- loss: float32 [], replicated
The draws below stay inside these ranges and needn't reach their ends.
Inputs may be any that keep to these rules, and one draw needn't show every extreme that they name: layer_input_rows rows and features carry varied scales.
All inputs are finite; a program needn't handle non-finite values.
Results may differ from the reference program's by a relative error of at most 0.0057.
Values may be sent and summed in bfloat16 or wider, within the bound.
No kernel may reach another device: no remote copies, remote signals or barrier semaphores. Data moves between devices by JAX's collectives and lax.ppermute only.
A program may use at most 128 MiB of HBM per device.

```python
import jax
import jax.numpy as jnp
from jax import lax

MODEL_WIDTH = 8192
ADAPTER_RANK = 64
KEY_VALUE_COLS = 1024
GROUP_TOKENS = 32768
TOKENS = 131072
N_GRP = 4


def draw_layer_input_rows(key, part):
    key_noise = jax.random.fold_in(key, 11)
    key_rows = jax.random.fold_in(key, 12)
    key_cols = jax.random.fold_in(key, 13)
    row_scale = jnp.exp(jax.random.uniform(key_rows, (TOKENS, 1), jnp.float32) * jnp.log(10.0))
    col_scale = jnp.exp(jax.random.uniform(key_cols, (1, MODEL_WIDTH), jnp.float32) * jnp.log(10.0))
    noise = jnp.clip(jax.random.normal(key_noise, (TOKENS, MODEL_WIDTH), jnp.float32), -4.0, 4.0)
    return (noise * row_scale * col_scale).astype(jnp.bfloat16)


def draw_target(key, part):
    key_noise = jax.random.fold_in(key, 21)
    position = jnp.arange(TOKENS, dtype=jnp.float32) / TOKENS
    growth = 1.0 + 2.0 * position
    noise = jnp.clip(jax.random.normal(key_noise, (TOKENS, KEY_VALUE_COLS), jnp.float32), -6.0, 6.0)
    return (noise * growth[:, None]).astype(jnp.bfloat16)


def set_ends(result, own_key, low, high):
    longest = result.shape.index(max(result.shape))
    spots = []
    for shift in (0, 1):
        where = [jax.random.randint(jax.random.fold_in(own_key, axis), (), 0, length) for axis, length in enumerate(result.shape)]
        where[longest] = (where[longest] + shift) % result.shape[longest]
        spots.append(tuple(where))
    return result.at[spots[0]].set(low).at[spots[1]].set(high)


def centred(rng, dims, deviation, reach, kind=jnp.bfloat16):
    return jnp.clip(deviation * jax.random.normal(rng, dims, jnp.float32), -reach, reach).astype(kind)


def setup_inputs(seed: int = 0) -> dict:
    seeds = jax.random.split(jax.random.key(seed), 9)
    return {
        "layer_input_rows": draw_layer_input_rows(jax.random.fold_in(seeds[8], 71), 0),
        "input_norm_gain": jnp.clip(1.0 + 0.1 * jax.random.normal(seeds[1], (MODEL_WIDTH,), jnp.float32), 0.5, 1.5).astype(jnp.bfloat16),
        "key_value_codes": set_ends(jax.random.randint(seeds[2], (MODEL_WIDTH, KEY_VALUE_COLS // 4), 0, 65536), jax.random.fold_in(seeds[2], 1), 0, 65535).astype(jnp.int32),
        "block_scale_codes": set_ends(jax.random.randint(seeds[3], (MODEL_WIDTH * KEY_VALUE_COLS // 32768, 128), -2147483648, 2147483647), jax.random.fold_in(seeds[3], 1), -2147483648, 2147483646).astype(jnp.int32),
        "outer_scale_codes": set_ends(jax.random.randint(seeds[4], (MODEL_WIDTH * KEY_VALUE_COLS // 16384,), 0, 256), jax.random.fold_in(seeds[4], 1), 0, 255).astype(jnp.int32),
        "adapter_down_factor": centred(seeds[5], (MODEL_WIDTH, ADAPTER_RANK), MODEL_WIDTH ** -0.5, 0.0625),
        "adapter_up_factor": centred(seeds[6], (ADAPTER_RANK, KEY_VALUE_COLS), ADAPTER_RANK ** -0.5, 0.75),
        "target": draw_target(jax.random.fold_in(seeds[8], 71), 0),
    }


adapter_scale = 0.25
epsilon = 1e-06
nf4_levels = (-1.0, -0.6961928009986877, -0.5250730514526367, -0.39491748809814453, -0.28444138169288635, -0.18477343022823334, -0.09105003625154495, 0.0, 0.07958029955625534, 0.16093020141124725, 0.24611230194568634, 0.33791524171066284, 0.44070982933044434, 0.5626170039176941, 0.7229568362236023, 1.0)

def unpack_scales(code_words, outer_scale_codes, all_rows):
    per_row = code_words.size // all_rows
    flat = code_words.reshape(all_rows, per_row)
    shifts = jnp.arange(4, dtype=jnp.int32) * 8
    code_bytes = jnp.bitwise_and(jnp.right_shift(flat[:, :, None], shifts[None, None, :]), 255)
    code_bytes = code_bytes.reshape(all_rows, per_row * 4).astype(jnp.float32)
    group_rows = all_rows // outer_scale_codes.shape[0]
    second = jnp.exp2(outer_scale_codes.astype(jnp.float32) / 128.0 - 6.0)
    second = jnp.repeat(second, group_rows)
    return (code_bytes + 0.5) / 256.0 * second[:, None]

def decode_codes(words, absmax):
    height = words.shape[0]
    shifts = jnp.arange(4, dtype=jnp.int32) * 4
    nibbles = jnp.bitwise_and(jnp.right_shift(words[:, :, None], shifts[None, None, :]), 15)
    nibbles = nibbles.reshape(height, words.shape[1] * 4)
    values = jnp.zeros(nibbles.shape, jnp.float32)
    for number, level in enumerate(nf4_levels):
        values = jnp.where(nibbles == number, jnp.float32(level), values)
    width = values.shape[1]
    count = absmax.shape[1]
    scaled = values.reshape(height, count, width // count) * absmax[:, :, None]
    return scaled.reshape(height, width).astype(jnp.bfloat16)

def apply_input_norm(input_states, input_norm_gain):
    values = input_states.astype(jnp.float32)
    inverse = lax.rsqrt(lax.optimization_barrier(jnp.mean(values * values, axis=1, keepdims=True)) + epsilon)
    return (values * inverse * input_norm_gain.astype(jnp.float32)[None, :]).astype(jnp.bfloat16)

def key_value_project(normed_input, decoded_weight, adapter_down_factor, adapter_up_factor):
    frozen_output = jnp.dot(normed_input, decoded_weight, preferred_element_type=jnp.float32)
    adapter_output = jnp.dot(normed_input, adapter_down_factor, preferred_element_type=jnp.float32).astype(jnp.bfloat16)
    return frozen_output + adapter_scale * jnp.dot(adapter_output, adapter_up_factor, preferred_element_type=jnp.float32)

def reference(layer_input_rows, input_norm_gain, key_value_codes, block_scale_codes, outer_scale_codes, adapter_down_factor, adapter_up_factor, target):
    absmax = unpack_scales(block_scale_codes, outer_scale_codes, key_value_codes.shape[0])
    decoded_weight = decode_codes(key_value_codes, absmax)

    def one_group(pair):
        input_states, teacher = pair
        precise_output = key_value_project(apply_input_norm(input_states, input_norm_gain), decoded_weight, adapter_down_factor, adapter_up_factor)
        error_terms = precise_output - teacher.astype(jnp.float32)
        return (precise_output.astype(jnp.bfloat16), jnp.sum(error_terms * error_terms) / (GROUP_TOKENS * KEY_VALUE_COLS))
    kv_out, losses = lax.map(one_group, (layer_input_rows.reshape(N_GRP, GROUP_TOKENS, MODEL_WIDTH), target.reshape(N_GRP, GROUP_TOKENS, KEY_VALUE_COLS)))
    return (kv_out.reshape(TOKENS, KEY_VALUE_COLS), jnp.sum(losses))
```

```python
import functools

import numpy as np

import jax
import jax.numpy as jnp
from jax import lax
from jax.experimental import pallas as pl
from jax.experimental.pallas import tpu as pltpu
from jax.sharding import PartitionSpec as P

adapter_scale = 0.25
epsilon = 1e-06
nf4_levels = (
    -1.0,
    -0.6961928009986877,
    -0.5250730514526367,
    -0.39491748809814453,
    -0.28444138169288635,
    -0.18477343022823334,
    -0.09105003625154495,
    0.0,
    0.07958029955625534,
    0.16093020141124725,
    0.24611230194568634,
    0.33791524171066284,
    0.44070982933044434,
    0.5626170039176941,
    0.7229568362236023,
    1.0,
)

AXES = ("grp", "fsdp")
LANES = 128
PART = 256
HALF = 2 * PART


def permutation(move):
    sizes = (2, 2, 4, 4, 4)
    pairs = []
    for source in range(int(np.prod(sizes))):
        place = [int(v) for v in np.unravel_index(source, sizes)]
        target = [v % s for v, s in zip(move(*place), sizes)]
        pairs.append((source, int(np.ravel_multi_index(target, sizes))))
    return pairs


def along(axis, step):
    def move(*place):
        place = list(place)
        place[axis] += step if place[1] == 0 else -step
        return place

    return permutation(move)


ZH, X, Y = 2, 3, 4
FORWARD = {axis: along(axis, 1) for axis in (ZH, X, Y)}
BACKWARD = {axis: along(axis, -1) for axis in (ZH, X, Y)}
ORDER = ((Y, X), (X, Y))
OTHER_CORE = permutation(lambda zl, c, zh, x, y: (zl, 1 - c, zh, x, y))


def ring(block, axis):
    behind = lax.ppermute(block, AXES, FORWARD[axis])
    ahead = lax.ppermute(block, AXES, BACKWARD[axis])
    opposite = lax.ppermute(behind, AXES, FORWARD[axis])
    return [block, behind, ahead, opposite]


_DEVICES = np.arange(256).reshape(16, 16)
LOSS_GROUPS = (_DEVICES.tolist(), _DEVICES.T.tolist())


def decode_kernel(place, outer, words, scale_words, gain, down, up, whole, levels):
    core = place[0]
    words_t = jnp.transpose(words[...])
    for j in range(4):
        code = jnp.bitwise_and(jnp.right_shift(words_t, 4 * j), 15)
        value = jnp.full(code.shape, nf4_levels[0], jnp.float32)
        for number in range(1, 16):
            value = jnp.where(code == number, jnp.float32(nf4_levels[number]), value)
        levels[pl.ds(j, LANES, stride=4), :] = value
    row = lax.broadcasted_iota(jnp.int32, (1, LANES), 1)
    second = jnp.zeros((1, LANES), jnp.float32)
    for g in range(8):
        code = outer[g].astype(jnp.float32)
        second = jnp.where(row // 16 == g, code, second)
    second = jnp.exp2(second / 128.0 - 6.0)
    code_bytes = jnp.concatenate(
        [
            jnp.bitwise_and(jnp.right_shift(scale_words[...], 8 * j), 255).astype(jnp.float32)
            for j in range(4)
        ],
        axis=0,
    ).astype(jnp.bfloat16)
    word_at = lax.broadcasted_iota(jnp.int32, (LANES, LANES), 0)
    row_at = lax.broadcasted_iota(jnp.int32, (LANES, LANES), 1)
    which = lax.broadcasted_iota(jnp.int32, (4, LANES), 0)
    own_rows = which == lax.broadcasted_iota(jnp.int32, (4, LANES), 1) // 32
    adapter = lax.dot_general(
        up[...], down[...], (((0,), (0,)), ((), ())), preferred_element_type=jnp.float32
    )
    gain_row = gain[0].astype(jnp.float32)
    pieces = []
    for q in range(2):
        pick = (word_at == 4 * (row_at % 32) + (2 * core + q)).astype(jnp.float32)
        found = jnp.dot(
            code_bytes, pick.astype(jnp.bfloat16), preferred_element_type=jnp.float32
        )
        for j in range(4):
            code = jnp.sum(
                jnp.where(own_rows, found[4 * j : 4 * j + 4], 0.0), axis=0, keepdims=True
            )
            absmax = (code + 0.5) / 256.0 * second
            block = 4 * q + j
            rows = slice(64 * block, 64 * block + 64)
            weight = levels[rows, :] * absmax + adapter_scale * adapter[rows]
            pieces.append((weight * gain_row).astype(jnp.bfloat16))
    whole[...] = jnp.concatenate(pieces, axis=0)


def decode(place, words, scale_words, outer, gain, down, up):
    grid = pltpu.PrefetchScalarGridSpec(
        num_scalar_prefetch=2,
        grid=(1,),
        in_specs=[
            pl.BlockSpec((LANES, LANES), lambda i, p, o: (0, p[0])),
            pl.BlockSpec((4, LANES), lambda i, p, o: (0, 0)),
            pl.BlockSpec((1, 1, LANES), lambda i, p, o: (p[1], 0, 0)),
            pl.BlockSpec((64, LANES), lambda i, p, o: (0, p[1])),
            pl.BlockSpec((64, HALF), lambda i, p, o: (0, p[0])),
        ],
        out_specs=pl.BlockSpec((HALF, LANES), lambda i, p, o: (0, 0)),
        scratch_shapes=[pltpu.VMEM((HALF, LANES), jnp.float32)],
    )
    return pl.pallas_call(
        decode_kernel,
        grid_spec=grid,
        out_shape=jax.ShapeDtypeStruct((HALF, LANES), jnp.bfloat16),
    )(place, outer, words, scale_words, gain.reshape(64, 1, LANES), down.T, up)


def ring_offset(core, j):
    step = 1 - 2 * core
    return jnp.where(j == 0, 0, jnp.where(j == 1, -step, jnp.where(j == 2, step, 2)))


def squares_kernel(x, squares):
    def rows(i, carry):
        at = pl.ds(pl.multiple_of(i * 16, 16), 16)
        sums = jnp.zeros((16, LANES), jnp.float32)
        for k in range(x.shape[1] // LANES):
            v = x[at, k * LANES : (k + 1) * LANES].astype(jnp.float32)
            sums += v * v
        squares[at, :] = sums
        return carry

    lax.fori_loop(0, x.shape[0] // 16, rows, 0)


def sum_squares(x):
    tokens, width = x.shape
    return pl.pallas_call(
        squares_kernel,
        grid=(8,),
        in_specs=[pl.BlockSpec((tokens // 8, width), lambda i: (i, 0))],
        out_specs=pl.BlockSpec((tokens // 8, LANES), lambda i: (i, 0)),
        out_shape=jax.ShapeDtypeStruct((tokens, LANES), jnp.float32),
        cost_estimate=pl.CostEstimate(
            flops=2 * tokens * width, transcendentals=0, bytes_accessed=2 * tokens * width
        ),
    )(x)


class Products:
    def __init__(self, arrivals, x, weights, x_space, w_space, x_sem, w_sem):
        core = lax.axis_index("grp") % 2
        own = lax.axis_index("fsdp")
        position = {ZH: own // 16, X: (own // 4) % 4, Y: own % 4}
        stride = {ZH: 16, X: 4, Y: 1}

        def base(axis, j):
            return (position[axis] + ring_offset(core, j)) % 4 * stride[axis]

        self.x_space, self.w_space, self.x_sem, self.w_sem = x_space, w_space, x_sem, w_sem
        self.weights = weights
        self.chunks = [(j, part) for j in arrivals for part in range(2)]
        tokens = x[0].shape[0]
        for chunk, (j, part) in enumerate(self.chunks):
            self.weight_copy(chunk).start()
            middle, last = ORDER[part]
            width = 4 * LANES if middle == Y else LANES
            for spot in range(0, 16 * LANES, width):
                shard = spot // (4 * LANES) * 16 + spot // LANES % 4 * stride[middle]
                source = pl.multiple_of((shard + base(last, j)) * LANES, LANES)
                for half in range(2):
                    pltpu.make_async_copy(
                        x[half].at[:, pl.ds(source, width)],
                        x_space.at[chunk, pl.ds(half * tokens, tokens), pl.ds(spot, width)],
                        x_sem.at[chunk],
                    ).start()

        def slot(axis, place):
            ahead = (place - position[axis]) % 4
            step = (1 - 2 * core) % 4
            return jnp.where(
                ahead == 0, 0, jnp.where(ahead == 2, 3, jnp.where(ahead == step, 2, 1))
            )

        self.slots = [
            [slot(middle, m) * 4 + slot(ZH, zh) for zh in range(4) for m in range(4)]
            for middle, _ in ORDER
        ]

    def weight_copy(self, chunk):
        return pltpu.make_async_copy(
            self.weights[chunk], self.w_space.at[chunk], self.w_sem.at[chunk]
        )

    def wait(self, chunk):
        space = self.x_space.at[chunk]
        pltpu.make_async_copy(space, space, self.x_sem.at[chunk]).wait()
        self.weight_copy(chunk).wait()

    def product(self, chunk, rows):
        slots = self.slots[self.chunks[chunk][1]]
        right = jnp.concatenate([self.w_space[chunk, slot] for slot in slots], axis=1)
        return lax.dot_general(
            self.x_space[chunk, rows, :],
            right,
            (((1,), (1,)), ((), ())),
            preferred_element_type=jnp.float32,
        )


ROWS = 256


def add_kernel(arrivals, *refs):
    first = 0 in arrivals
    count = 2 * len(arrivals)
    x, refs = refs[:2], refs[2:]
    weights, refs = refs[:count], refs[count:]
    if not first:
        before, refs = refs[0], refs[1:]
    out, x_space, w_space, total, x_sem, w_sem, sem = refs
    if not first:
        bring = pltpu.make_async_copy(before, total, sem)
        bring.start()
    products = Products(arrivals, x, weights, x_space, w_space, x_sem, w_sem)
    if not first:
        bring.wait()
    for chunk, (j, part) in enumerate(products.chunks):
        products.wait(chunk)
        columns = slice(part * PART, (part + 1) * PART)

        def step(i, carry, chunk=chunk, columns=columns, fresh=j == 0):
            rows = pl.ds(pl.multiple_of(i * ROWS, ROWS), ROWS)
            value = products.product(chunk, rows)
            if not fresh:
                value += total[rows, columns]
            total[rows, columns] = value
            return carry

        lax.fori_loop(0, total.shape[0] // ROWS, step, 0)
    give = pltpu.make_async_copy(total, out, sem)
    give.start()
    give.wait()


def last_kernel(
    x0, x1, wb, wc, before, squares0, squares1, t0, t1,
    kv, other_kv, errors,
    x_space, w_space, total, squares, targets, halves, x_sem, w_sem, sems,
):
    core = lax.axis_index("grp") % 2
    tokens, width = x0.shape
    brought = []
    for i, (source, space) in enumerate(
        (
            (before, total),
            (squares0, squares.at[:tokens]),
            (squares1, squares.at[tokens:]),
            (t0, targets.at[:tokens]),
            (t1, targets.at[tokens:]),
        )
    ):
        brought.append(pltpu.make_async_copy(source, space, sems.at[i]))
        brought[-1].start()
    products = Products((3,), (x0, x1), (wb, wc), x_space, w_space, x_sem, w_sem)
    for copy in brought:
        copy.wait()
    errors[...] = jnp.zeros_like(errors)
    for chunk in range(2):
        products.wait(chunk)

    def step(i, carry):
        rows = pl.ds(pl.multiple_of(i * ROWS, ROWS), ROWS)
        mean = jnp.sum(squares[rows, :], axis=1, keepdims=True) / width
        scale = lax.rsqrt(mean + epsilon)
        for part in range(2):
            columns = slice(part * PART, (part + 1) * PART)
            exact = (total[rows, columns] + products.product(part, rows)) * scale
            halves[rows, columns] = exact.astype(jnp.bfloat16)
            error = exact - targets[rows, columns].astype(jnp.float32)
            error = error * error
            error = error[:, :LANES] + error[:, LANES:]
            errors[...] += jnp.sum(error.reshape(ROWS // 8, 8, LANES), axis=0)
        return carry

    lax.fori_loop(0, total.shape[0] // ROWS, step, 0)
    at = pl.multiple_of(core * HALF, HALF)
    copies = [
        pltpu.make_async_copy(halves.at[tokens:], other_kv, sems.at[0]),
        pltpu.make_async_copy(halves.at[:tokens], kv.at[:, pl.ds(at, HALF)], sems.at[1]),
    ]
    for copy in copies:
        copy.start()
    for copy in copies:
        copy.wait()


ANY = pl.BlockSpec(memory_space=pl.ANY)
HBM = pl.BlockSpec(memory_space=pltpu.HBM)
VMEM = pl.BlockSpec(memory_space=pltpu.VMEM)


def params(mib):
    return pltpu.CompilerParams(vmem_limit_bytes=mib << 20)


def cost(tokens, chunks):
    depth = 16 * LANES
    return pl.CostEstimate(
        flops=2 * chunks * 2 * tokens * depth * PART,
        transcendentals=0,
        bytes_accessed=chunks * (4 * tokens + 2 * PART) * depth + 16 * tokens * HALF,
    )


def shape(dims, kind):
    return jax.ShapeDtypeStruct(dims, kind)


def spaces(chunks, tokens):
    return [
        pltpu.VMEM((chunks, 2 * tokens, 16 * LANES), jnp.bfloat16),
        pltpu.VMEM((chunks, 16, PART, LANES), jnp.bfloat16),
        pltpu.VMEM((2 * tokens, HALF), jnp.float32),
    ]


def semaphores(chunks):
    return [pltpu.SemaphoreType.DMA((chunks,)), pltpu.SemaphoreType.DMA((chunks,))]


def add(arrivals, x, weights, before):
    tokens = x[0].shape[0]
    flat = [w for pair in weights for w in pair]
    operands = [*x, *flat] + ([] if before is None else [before])
    return pl.pallas_call(
        functools.partial(add_kernel, arrivals),
        in_specs=[HBM] * 2 + [ANY] * (len(operands) - 2),
        out_specs=ANY,
        out_shape=shape((2 * tokens, HALF), jnp.float32),
        scratch_shapes=spaces(len(flat), tokens)
        + semaphores(len(flat))
        + [pltpu.SemaphoreType.DMA(())],
        compiler_params=params(12 * len(flat) // 2 + 4),
        cost_estimate=cost(tokens, len(flat)),
    )(*operands)


def finish(x, weights, before, squares, targets):
    tokens = x[0].shape[0]
    return pl.pallas_call(
        last_kernel,
        in_specs=[HBM] * 2 + [ANY] * 7,
        out_specs=[ANY, ANY, VMEM],
        out_shape=[
            shape((tokens, 2 * HALF), jnp.bfloat16),
            shape((tokens, HALF), jnp.bfloat16),
            shape((8, LANES), jnp.float32),
        ],
        scratch_shapes=spaces(2, tokens)
        + [
            pltpu.VMEM((2 * tokens, LANES), jnp.float32),
            pltpu.VMEM((2 * tokens, HALF), jnp.bfloat16),
            pltpu.VMEM((2 * tokens, HALF), jnp.bfloat16),
        ]
        + semaphores(2)
        + [pltpu.SemaphoreType.DMA((5,))],
        compiler_params=params(24),
        cost_estimate=cost(tokens, 2),
    )(*x, *weights, before, *squares, *targets)


def sum_over(value, groups):
    length = len(groups[0])
    everything = lax.all_to_all(
        jnp.broadcast_to(value[None], (length,)), AXES, 0, 0, axis_index_groups=groups, tiled=True
    )
    return jnp.sum(everything)


def per_device(
    layer_input_rows,
    input_norm_gain,
    key_value_codes,
    block_scale_codes,
    outer_scale_codes,
    adapter_down_factor,
    adapter_up_factor,
    target,
):
    core = lax.axis_index("grp") % 2
    shard = lax.axis_index("fsdp")

    tokens = layer_input_rows.shape[0]
    other_rows = lax.ppermute(layer_input_rows, AXES, OTHER_CORE)
    own_target = lax.dynamic_slice(target, (0, core * HALF), (tokens, HALF))
    other_target = lax.ppermute(
        lax.dynamic_slice(target, (0, (1 - core) * HALF), (tokens, HALF)), AXES, OTHER_CORE
    )

    own_weight = decode(
        jnp.stack([core, shard]),
        key_value_codes,
        block_scale_codes,
        outer_scale_codes,
        input_norm_gain,
        adapter_down_factor,
        adapter_up_factor,
    )
    along_z = ring(own_weight, ZH)
    planes = []
    for part, (middle, last) in enumerate(ORDER):
        columns = slice(part * PART, (part + 1) * PART)
        line = jnp.stack([piece[columns] for piece in along_z])
        planes.append(jnp.concatenate(ring(line, middle)))

    behind = [lax.ppermute(p, AXES, FORWARD[last]) for p, (_, last) in zip(planes, ORDER)]
    ahead = [lax.ppermute(p, AXES, BACKWARD[last]) for p, (_, last) in zip(planes, ORDER)]
    own_rows, other_rows, *planes = lax.optimization_barrier(
        (layer_input_rows, other_rows, *planes)
    )
    x = (own_rows, other_rows)
    total = add((0,), x, [planes], None)
    own_squares = sum_squares(own_rows)
    total, own_squares, *behind = lax.optimization_barrier((total, own_squares, *behind))
    squares = (own_squares, lax.ppermute(own_squares, AXES, OTHER_CORE))
    opposite = [lax.ppermute(p, AXES, FORWARD[last]) for p, (_, last) in zip(behind, ORDER)]
    total = add((1, 2), x, [behind, ahead], total)
    kv, other_kv, errors = finish(x, opposite, total, squares, (own_target, other_target))
    received = lax.ppermute(other_kv, AXES, OTHER_CORE)
    kv = lax.dynamic_update_slice(kv, received, (0, (1 - core) * HALF))

    loss = jnp.sum(errors) / (tokens * lax.axis_size("fsdp") * 2 * HALF)
    for groups in LOSS_GROUPS:
        loss = sum_over(loss, groups)
    return kv, loss


def solution(mesh):
    placed = (
        P(("grp", "fsdp"), None),
        P(),
        P("fsdp", None),
        P("fsdp", None),
        P("fsdp"),
        P(),
        P(),
        P(("grp", "fsdp"), None),
    )
    return jax.shard_map(
        per_device,
        mesh=mesh,
        in_specs=placed,
        out_specs=(P(("grp", "fsdp"), None), P()),
        check_vma=False,
    )
```

```python
import functools

import numpy as np

import jax
import jax.numpy as jnp
from jax import lax
from jax.experimental import pallas as pl
from jax.experimental.pallas import tpu as pltpu
from jax.sharding import PartitionSpec as P

adapter_scale = 0.25
epsilon = 1e-06
nf4_levels = (
    -1.0,
    -0.6961928009986877,
    -0.5250730514526367,
    -0.39491748809814453,
    -0.28444138169288635,
    -0.18477343022823334,
    -0.09105003625154495,
    0.0,
    0.07958029955625534,
    0.16093020141124725,
    0.24611230194568634,
    0.33791524171066284,
    0.44070982933044434,
    0.5626170039176941,
    0.7229568362236023,
    1.0,
)

AXES = ("grp", "fsdp")
LANES = 128
PART = 256
HALF = 2 * PART


def permutation(move):
    sizes = (2, 2, 4, 4, 4)
    pairs = []
    for source in range(int(np.prod(sizes))):
        place = [int(v) for v in np.unravel_index(source, sizes)]
        target = [v % s for v, s in zip(move(*place), sizes)]
        pairs.append((source, int(np.ravel_multi_index(target, sizes))))
    return pairs


def along(axis, step):
    def move(*place):
        place = list(place)
        place[axis] += step if place[1] == 0 else -step
        return place

    return permutation(move)


ZH, X, Y = 2, 3, 4
FORWARD = {axis: along(axis, 1) for axis in (ZH, X, Y)}
BACKWARD = {axis: along(axis, -1) for axis in (ZH, X, Y)}
ORDER = ((Y, X), (X, Y))
STRIDE = {ZH: 16, X: 4, Y: 1}
ACROSS_ZH = permutation(lambda zl, c, zh, x, y: (1 - zl, c, zh + 2, x, y))
OTHER_CORE = permutation(lambda zl, c, zh, x, y: (zl, 1 - c, zh, x, y))


def ring(block, axis):
    behind = lax.ppermute(block, AXES, FORWARD[axis])
    ahead = lax.ppermute(block, AXES, BACKWARD[axis])
    if axis == ZH:
        opposite = lax.ppermute(block, AXES, ACROSS_ZH)
    else:
        opposite = lax.ppermute(behind, AXES, FORWARD[axis])
    return [block, behind, ahead, opposite]


_DEVICES = np.arange(256).reshape(2, 2, 4, 16).transpose(0, 2, 1, 3).reshape(8, 32)
LOSS_GROUPS = (_DEVICES.tolist(), _DEVICES.T.tolist())


ANY = pl.BlockSpec(memory_space=pl.ANY)
VMEM = pl.BlockSpec(memory_space=pltpu.VMEM)
SMEM = pl.BlockSpec(memory_space=pltpu.SMEM)


def shape(dims, kind):
    return jax.ShapeDtypeStruct(dims, kind)


def params(mib):
    return pltpu.CompilerParams(vmem_limit_bytes=mib << 20)


def decode_kernel(
    outer, words, scale_words, gain, down, up, whole, levels, own_words, own_down, own_up, sems
):
    core = lax.axis_index("grp") % 2
    shard = lax.axis_index("fsdp")
    lanes = pl.ds(pl.multiple_of(core * LANES, LANES), LANES)
    rows = pl.ds(pl.multiple_of(shard * LANES, LANES), LANES)
    half = pl.ds(pl.multiple_of(core * HALF, HALF), HALF)
    copies = [
        pltpu.make_async_copy(words.at[:, lanes], own_words, sems.at[0]),
        pltpu.make_async_copy(down.at[:, rows], own_down, sems.at[1]),
        pltpu.make_async_copy(up.at[:, half], own_up, sems.at[2]),
    ]
    for copy in copies:
        copy.start()
    for copy in copies:
        copy.wait()
    words_t = jnp.transpose(own_words[...])
    for j in range(4):
        code = jnp.bitwise_and(jnp.right_shift(words_t, 4 * j), 15)
        value = jnp.full(code.shape, nf4_levels[0], jnp.float32)
        for number in range(1, 16):
            value = jnp.where(code == number, jnp.float32(nf4_levels[number]), value)
        levels[pl.ds(j, LANES, stride=4), :] = value
    row = lax.broadcasted_iota(jnp.int32, (1, LANES), 1)
    second = jnp.zeros((1, LANES), jnp.float32)
    for g in range(8):
        code = outer[g].astype(jnp.float32)
        second = jnp.where(row // 16 == g, code, second)
    second = jnp.exp2(second / 128.0 - 6.0)
    code_bytes = jnp.concatenate(
        [
            jnp.bitwise_and(jnp.right_shift(scale_words[...], 8 * j), 255).astype(jnp.float32)
            for j in range(4)
        ],
        axis=0,
    ).astype(jnp.bfloat16)
    word_at = lax.broadcasted_iota(jnp.int32, (LANES, LANES), 0)
    row_at = lax.broadcasted_iota(jnp.int32, (LANES, LANES), 1)
    which = lax.broadcasted_iota(jnp.int32, (4, LANES), 0)
    own_rows = which == lax.broadcasted_iota(jnp.int32, (4, LANES), 1) // 32
    adapter = lax.dot_general(
        own_up[...], own_down[...], (((0,), (0,)), ((), ())), preferred_element_type=jnp.float32
    )
    gains = gain[...].astype(jnp.float32).reshape(64, LANES)
    is_own = lax.broadcasted_iota(jnp.int32, gains.shape, 0) == shard
    gain_row = jnp.sum(jnp.where(is_own, gains, 0.0), axis=0, keepdims=True)
    pieces = []
    for q in range(2):
        pick = (word_at == 4 * (row_at % 32) + (2 * core + q)).astype(jnp.float32)
        found = jnp.dot(
            code_bytes, pick.astype(jnp.bfloat16), preferred_element_type=jnp.float32
        )
        for j in range(4):
            code = jnp.sum(
                jnp.where(own_rows, found[4 * j : 4 * j + 4], 0.0), axis=0, keepdims=True
            )
            absmax = (code + 0.5) / 256.0 * second
            block = 4 * q + j
            rows = slice(64 * block, 64 * block + 64)
            weight = levels[rows, :] * absmax + adapter_scale * adapter[rows]
            pieces.append((weight * gain_row).astype(jnp.bfloat16))
    whole[...] = jnp.concatenate(pieces, axis=0)


def decode(words, scale_words, outer, gain, down, up):
    return pl.pallas_call(
        decode_kernel,
        in_specs=[SMEM, ANY, VMEM, VMEM, ANY, ANY],
        out_specs=VMEM,
        out_shape=shape((HALF, LANES), jnp.bfloat16),
        scratch_shapes=[
            pltpu.VMEM((HALF, LANES), jnp.float32),
            pltpu.VMEM((LANES, LANES), jnp.int32),
            pltpu.VMEM((64, LANES), jnp.bfloat16),
            pltpu.VMEM((64, HALF), jnp.bfloat16),
            pltpu.SemaphoreType.DMA((3,)),
        ],
    )(outer, words, scale_words, gain, down.T, up)


def ring_offset(core, j):
    step = 1 - 2 * core
    return jnp.where(j == 0, 0, jnp.where(j == 1, -step, jnp.where(j == 2, step, 2)))


ROWS = 256
STEPS = 4


class Layout:
    def __init__(self, place):
        self.core, own = place[0], place[1]
        self.position = {ZH: own // 16, X: (own // 4) % 4, Y: own % 4}

    def features(self, arrival, part):
        middle, last = ORDER[part]
        at = (self.position[last] + ring_offset(self.core, arrival)) % 4 * STRIDE[last]
        width = 4 if middle == Y else 1
        for spot in range(0, 16, width):
            shard = spot // 4 * 16 + spot % 4 * STRIDE[middle] + at
            yield pl.multiple_of(shard * LANES, width * LANES), width * LANES

    def slots(self, part):
        middle, _ = ORDER[part]

        def slot(axis, place):
            ahead = (place - self.position[axis]) % 4
            step = (1 - 2 * self.core) % 4
            return jnp.where(
                ahead == 0, 0, jnp.where(ahead == 2, 3, jnp.where(ahead == step, 2, 1))
            )

        return [slot(middle, m) * 4 + slot(ZH, zh) for zh in range(4) for m in range(4)]


def product(left, weight, slots):
    right = jnp.concatenate([weight[slot] for slot in slots], axis=1)
    return lax.dot_general(
        left, right, (((1,), (1,)), ((), ())), preferred_element_type=jnp.float32
    )


def rows_of(width):
    return pl.BlockSpec((ROWS, width), lambda i, place: (i, 0))


def by_core(place):
    return place[0]


def rows_of_own(width, column=lambda place: 0):
    return pl.BlockSpec(
        (ROWS, width), lambda i, place: (jnp.minimum(i, STEPS // 2 - 1), column(place))
    )


def rows_of_other(width, column=lambda place: 0):
    return pl.BlockSpec(
        (ROWS, width), lambda i, place: (jnp.maximum(i - STEPS // 2, 0), column(place))
    )


def whole_weight():
    return pl.BlockSpec((16, PART, LANES), lambda i, place: (0, 0, 0))


def on_own_or_other(own, other, body):
    @pl.when(pl.program_id(0) < STEPS // 2)
    def _():
        body(*own)

    @pl.when(pl.program_id(0) >= STEPS // 2)
    def _():
        body(*other)


def taken(x, layout, arrival, part):
    return jnp.concatenate(
        [x[:, pl.ds(*run)] for run in layout.features(arrival, part)], axis=1
    )


def first_kernel(place, x0, x1, wb, wc, total, last):
    layout = Layout(place)
    depth = 16 * LANES

    def body(x):
        for part, weight in enumerate((wb, wc)):
            columns = slice(part * PART, (part + 1) * PART)
            total[:, columns] = product(
                taken(x, layout, 0, part), weight, layout.slots(part)
            )
            at = part * depth
            for start, width in layout.features(3, part):
                last[:, at : at + width] = x[:, pl.ds(start, width)]
                at += width

    on_own_or_other((x0,), (x1,), body)


def squares_kernel(x, squares):
    sums = jnp.zeros(squares.shape, jnp.float32)
    for k in range(0, x.shape[1], LANES):
        v = x[:, k : k + LANES].astype(jnp.float32)
        sums += v * v
    squares[...] = sums


def sum_squares(x):
    tokens, width = x.shape
    return pl.pallas_call(
        squares_kernel,
        grid=(8,),
        in_specs=[pl.BlockSpec((tokens // 8, width), lambda i: (i, 0))],
        out_specs=pl.BlockSpec((tokens // 8, LANES), lambda i: (i, 0)),
        out_shape=shape((tokens, LANES), jnp.float32),
        compiler_params=params(58),
    )(x)


def estimate(tokens, chunks):
    depth = 16 * LANES
    return pl.CostEstimate(
        flops=4 * tokens * chunks * depth * PART,
        transcendentals=0,
        bytes_accessed=4 * tokens * chunks * depth + 16 * tokens * HALF,
    )


def first(place, x, weights):
    tokens, width = x[0].shape
    depth = 2 * 16 * LANES
    return pl.pallas_call(
        first_kernel,
        grid_spec=pltpu.PrefetchScalarGridSpec(
            num_scalar_prefetch=1,
            grid=(STEPS,),
            in_specs=[rows_of_own(width), rows_of_other(width)] + [whole_weight()] * 2,
            out_specs=[rows_of(HALF), rows_of(depth)],
        ),
        out_shape=[
            shape((2 * tokens, HALF), jnp.float32),
            shape((2 * tokens, depth), jnp.bfloat16),
        ],
        compiler_params=params(34),
        cost_estimate=estimate(tokens, 4),
    )(place, *x, *weights)


def next_kernel(place, x0, x1, wb1, wc1, wb2, wc2, before, total):
    layout = Layout(place)

    def body(x):
        for part, weights in enumerate(((wb1, wb2), (wc1, wc2))):
            columns = slice(part * PART, (part + 1) * PART)
            value = before[:, columns]
            for arrival, weight in enumerate(weights, 1):
                value += product(taken(x, layout, arrival, part), weight, layout.slots(part))
            total[:, columns] = value

    on_own_or_other((x0,), (x1,), body)


def following(place, x, weights, before):
    tokens, width = x[0].shape
    flat = [w for pair in weights for w in pair]
    return pl.pallas_call(
        next_kernel,
        grid_spec=pltpu.PrefetchScalarGridSpec(
            num_scalar_prefetch=1,
            grid=(STEPS,),
            in_specs=[rows_of_own(width), rows_of_other(width)]
            + [whole_weight()] * 4
            + [rows_of(HALF)],
            out_specs=rows_of(HALF),
        ),
        out_shape=shape((2 * tokens, HALF), jnp.float32),
        compiler_params=params(40),
        cost_estimate=estimate(tokens, 4),
    )(place, *x, *flat, before)


def last_kernel(
    place, x, wb, wc, before, squares0, squares1, t0, t1, kv, other_kv, errors, sums
):
    layout = Layout(place)
    step = pl.program_id(0)

    @pl.when(step == 0)
    def _():
        sums[...] = jnp.zeros_like(sums)

    width = 2 * x.shape[1]
    depth = 16 * LANES

    def body(squares, target, out):
        mean = jnp.sum(squares[...], axis=1, keepdims=True) / width
        scale = lax.rsqrt(mean + epsilon)
        for part, weight in enumerate((wb, wc)):
            columns = slice(part * PART, (part + 1) * PART)
            value = product(
                x[:, part * depth : (part + 1) * depth], weight, layout.slots(part)
            )
            exact = (before[:, columns] + value) * scale
            out[:, columns] = exact.astype(jnp.bfloat16)
            error = exact - target[:, columns].astype(jnp.float32)
            error = error * error
            error = error[:, :LANES] + error[:, LANES:]
            sums[...] += jnp.sum(error.reshape(-1, 8, LANES), axis=0)

    on_own_or_other((squares0, t0, kv), (squares1, t1, other_kv), body)

    @pl.when(step == STEPS - 1)
    def _():
        errors[...] = jnp.broadcast_to(jnp.sum(sums[...], axis=0, keepdims=True), errors.shape)


def finish(place, x, weights, before, squares, targets):
    tokens, depth = x.shape[0] // 2, x.shape[1]
    return pl.pallas_call(
        last_kernel,
        grid_spec=pltpu.PrefetchScalarGridSpec(
            num_scalar_prefetch=1,
            grid=(STEPS,),
            in_specs=[rows_of(depth)]
            + [whole_weight()] * 2
            + [rows_of(HALF)]
            + [rows_of_own(LANES), rows_of_other(LANES)]
            + [rows_of_own(HALF, by_core), rows_of_other(HALF, by_core)],
            out_specs=[
                rows_of_own(HALF, by_core),
                rows_of_other(HALF),
                pl.BlockSpec((32, LANES), lambda i, place: (0, 0)),
            ],
            scratch_shapes=[pltpu.VMEM((8, LANES), jnp.float32)],
        ),
        out_shape=[
            shape((tokens, 2 * HALF), jnp.bfloat16),
            shape((tokens, HALF), jnp.bfloat16),
            shape((32, LANES), jnp.float32),
        ],
        compiler_params=params(26),
        cost_estimate=estimate(tokens, 2),
    )(place, x, *weights, before, *squares, *targets)


def swap_rows(everyone, groups):
    return lax.all_to_all(everyone, AXES, 0, 0, axis_index_groups=groups, tiled=True)


def spread_kernel(rows, out):
    out[...] = jnp.broadcast_to(jnp.sum(rows[...], axis=0, keepdims=True), out.shape)


def per_device(
    layer_input_rows,
    input_norm_gain,
    key_value_codes,
    block_scale_codes,
    outer_scale_codes,
    adapter_down_factor,
    adapter_up_factor,
    target,
):
    core = lax.axis_index("grp") % 2
    shard = lax.axis_index("fsdp")

    tokens = layer_input_rows.shape[0]
    other_rows = lax.ppermute(layer_input_rows, AXES, OTHER_CORE)
    place = jnp.stack([core, shard]).astype(jnp.int32)
    other_target = lax.ppermute(target, AXES, OTHER_CORE)

    own_weight = decode(
        key_value_codes,
        block_scale_codes,
        outer_scale_codes,
        input_norm_gain,
        adapter_down_factor,
        adapter_up_factor,
    )
    own_rows, own_weight = lax.optimization_barrier((layer_input_rows, own_weight))
    own_squares = sum_squares(own_rows)
    along_z = ring(own_weight, ZH)
    own_squares, other_target, *along_z = lax.optimization_barrier(
        (own_squares, other_target, *along_z)
    )
    squares = (own_squares, lax.ppermute(own_squares, AXES, OTHER_CORE))
    planes = []
    for part, (middle, last) in enumerate(ORDER):
        columns = slice(part * PART, (part + 1) * PART)
        line = jnp.stack([piece[columns] for piece in along_z])
        planes.append(jnp.concatenate(ring(line, middle)))

    behind = [lax.ppermute(p, AXES, FORWARD[last]) for p, (_, last) in zip(planes, ORDER)]
    ahead = [lax.ppermute(p, AXES, BACKWARD[last]) for p, (_, last) in zip(planes, ORDER)]
    x = (layer_input_rows, other_rows)
    total, last_x = first(place, x, planes)
    total, *behind = lax.optimization_barrier((total, *behind))
    opposite = [lax.ppermute(p, AXES, FORWARD[last]) for p, (_, last) in zip(behind, ORDER)]
    total = following(place, x, [behind, ahead], total)
    kv, other_kv, errors = finish(
        place, last_x, opposite, total, squares, (target, other_target)
    )
    received = lax.ppermute(other_kv, AXES, OTHER_CORE)
    kv = lax.dynamic_update_slice(kv, received, (0, (1 - core) * HALF))

    sums = swap_rows(errors, LOSS_GROUPS[0])
    sums = pl.pallas_call(
        spread_kernel, in_specs=[VMEM], out_specs=VMEM, out_shape=shape((8, LANES), jnp.float32)
    )(sums)
    sums = swap_rows(sums, LOSS_GROUPS[1])
    loss = jnp.sum(sums) / (tokens * lax.axis_size("fsdp") * 2 * HALF)
    return kv, loss


def solution(mesh):
    placed = (
        P(("grp", "fsdp"), None),
        P(),
        P("fsdp", None),
        P("fsdp", None),
        P("fsdp"),
        P(),
        P(),
        P(("grp", "fsdp"), None),
    )
    return jax.shard_map(
        per_device,
        mesh=mesh,
        in_specs=placed,
        out_specs=(P(("grp", "fsdp"), None), P()),
        check_vma=False,
    )
```

```python
import functools

import numpy as np

import jax
import jax.numpy as jnp
from jax import lax
from jax.experimental import pallas as pl
from jax.experimental.pallas import tpu as pltpu
from jax.sharding import PartitionSpec as P

adapter_scale = 0.25
epsilon = 1e-06
nf4_levels = (
    -1.0,
    -0.6961928009986877,
    -0.5250730514526367,
    -0.39491748809814453,
    -0.28444138169288635,
    -0.18477343022823334,
    -0.09105003625154495,
    0.0,
    0.07958029955625534,
    0.16093020141124725,
    0.24611230194568634,
    0.33791524171066284,
    0.44070982933044434,
    0.5626170039176941,
    0.7229568362236023,
    1.0,
)

AXES = ("grp", "fsdp")
LANES = 128
PART = 256
HALF = 2 * PART


def permutation(move):
    sizes = (2, 2, 4, 4, 4)
    pairs = []
    for source in range(int(np.prod(sizes))):
        place = [int(v) for v in np.unravel_index(source, sizes)]
        target = [v % s for v, s in zip(move(*place), sizes)]
        pairs.append((source, int(np.ravel_multi_index(target, sizes))))
    return pairs


def along(axis, step):
    def move(*place):
        place = list(place)
        place[axis] += step if place[1] == 0 else -step
        return place

    return permutation(move)


ZH, X, Y = 2, 3, 4
FORWARD = {axis: along(axis, 1) for axis in (ZH, X, Y)}
BACKWARD = {axis: along(axis, -1) for axis in (ZH, X, Y)}
ORDER = ((Y, X), (X, Y))
STRIDE = {ZH: 16, X: 4, Y: 1}
ACROSS_ZH = permutation(lambda zl, c, zh, x, y: (1 - zl, c, zh + 2, x, y))
OTHER_CORE = permutation(lambda zl, c, zh, x, y: (zl, 1 - c, zh, x, y))


def ring(block, axis):
    behind = lax.ppermute(block, AXES, FORWARD[axis])
    ahead = lax.ppermute(block, AXES, BACKWARD[axis])
    if axis == ZH:
        opposite = lax.ppermute(block, AXES, ACROSS_ZH)
    else:
        opposite = lax.ppermute(behind, AXES, FORWARD[axis])
    return [block, behind, ahead, opposite]


_DEVICES = np.arange(256).reshape(2, 2, 4, 16).transpose(0, 2, 1, 3).reshape(8, 32)
LOSS_GROUPS = (_DEVICES.tolist(), _DEVICES.T.tolist())


ANY = pl.BlockSpec(memory_space=pl.ANY)
VMEM = pl.BlockSpec(memory_space=pltpu.VMEM)
SMEM = pl.BlockSpec(memory_space=pltpu.SMEM)


def shape(dims, kind):
    return jax.ShapeDtypeStruct(dims, kind)


def params(mib):
    return pltpu.CompilerParams(vmem_limit_bytes=mib << 20)


def decode_kernel(
    outer, words, scale_words, gain, down, up, whole, levels, own_words, own_down, own_up, sems
):
    core = lax.axis_index("grp") % 2
    shard = lax.axis_index("fsdp")
    lanes = pl.ds(pl.multiple_of(core * LANES, LANES), LANES)
    rows = pl.ds(pl.multiple_of(shard * LANES, LANES), LANES)
    half = pl.ds(pl.multiple_of(core * HALF, HALF), HALF)
    copies = [
        pltpu.make_async_copy(words.at[:, lanes], own_words, sems.at[0]),
        pltpu.make_async_copy(down.at[:, rows], own_down, sems.at[1]),
        pltpu.make_async_copy(up.at[:, half], own_up, sems.at[2]),
    ]
    for copy in copies:
        copy.start()
    for copy in copies:
        copy.wait()
    words_t = jnp.transpose(own_words[...])
    for j in range(4):
        code = jnp.bitwise_and(jnp.right_shift(words_t, 4 * j), 15)
        value = jnp.full(code.shape, nf4_levels[0], jnp.float32)
        for number in range(1, 16):
            value = jnp.where(code == number, jnp.float32(nf4_levels[number]), value)
        levels[pl.ds(j, LANES, stride=4), :] = value
    row = lax.broadcasted_iota(jnp.int32, (1, LANES), 1)
    second = jnp.zeros((1, LANES), jnp.float32)
    for g in range(8):
        code = outer[g].astype(jnp.float32)
        second = jnp.where(row // 16 == g, code, second)
    second = jnp.exp2(second / 128.0 - 6.0)
    code_bytes = jnp.concatenate(
        [
            jnp.bitwise_and(jnp.right_shift(scale_words[...], 8 * j), 255).astype(jnp.float32)
            for j in range(4)
        ],
        axis=0,
    ).astype(jnp.bfloat16)
    word_at = lax.broadcasted_iota(jnp.int32, (LANES, LANES), 0)
    row_at = lax.broadcasted_iota(jnp.int32, (LANES, LANES), 1)
    which = lax.broadcasted_iota(jnp.int32, (4, LANES), 0)
    own_rows = which == lax.broadcasted_iota(jnp.int32, (4, LANES), 1) // 32
    adapter = lax.dot_general(
        own_up[...], own_down[...], (((0,), (0,)), ((), ())), preferred_element_type=jnp.float32
    )
    gains = gain[...].astype(jnp.float32).reshape(64, LANES)
    is_own = lax.broadcasted_iota(jnp.int32, gains.shape, 0) == shard
    gain_row = jnp.sum(jnp.where(is_own, gains, 0.0), axis=0, keepdims=True)
    pieces = []
    for q in range(2):
        pick = (word_at == 4 * (row_at % 32) + (2 * core + q)).astype(jnp.float32)
        found = jnp.dot(
            code_bytes, pick.astype(jnp.bfloat16), preferred_element_type=jnp.float32
        )
        for j in range(4):
            code = jnp.sum(
                jnp.where(own_rows, found[4 * j : 4 * j + 4], 0.0), axis=0, keepdims=True
            )
            absmax = (code + 0.5) / 256.0 * second
            block = 4 * q + j
            rows = slice(64 * block, 64 * block + 64)
            weight = levels[rows, :] * absmax + adapter_scale * adapter[rows]
            pieces.append((weight * gain_row).astype(jnp.bfloat16))
    whole[...] = jnp.concatenate(pieces, axis=0)


def decode(words, scale_words, outer, gain, down, up):
    return pl.pallas_call(
        decode_kernel,
        in_specs=[SMEM, ANY, VMEM, VMEM, ANY, ANY],
        out_specs=VMEM,
        out_shape=shape((HALF, LANES), jnp.bfloat16),
        scratch_shapes=[
            pltpu.VMEM((HALF, LANES), jnp.float32),
            pltpu.VMEM((LANES, LANES), jnp.int32),
            pltpu.VMEM((64, LANES), jnp.bfloat16),
            pltpu.VMEM((64, HALF), jnp.bfloat16),
            pltpu.SemaphoreType.DMA((3,)),
        ],
    )(outer, words, scale_words, gain, down.T, up)


def ring_offset(core, j):
    step = 1 - 2 * core
    return jnp.where(j == 0, 0, jnp.where(j == 1, -step, jnp.where(j == 2, step, 2)))


ROWS = 256
STEPS = 4


class Layout:
    def __init__(self, place):
        self.core, own = place[0], place[1]
        self.position = {ZH: own // 16, X: (own // 4) % 4, Y: own % 4}

    def features(self, arrival, part):
        middle, last = ORDER[part]
        at = (self.position[last] + ring_offset(self.core, arrival)) % 4 * STRIDE[last]
        width = 4 if middle == Y else 1
        for spot in range(0, 16, width):
            shard = spot // 4 * 16 + spot % 4 * STRIDE[middle] + at
            yield pl.multiple_of(shard * LANES, width * LANES), width * LANES

    def slots(self, part):
        middle, _ = ORDER[part]

        def slot(axis, place):
            ahead = (place - self.position[axis]) % 4
            step = (1 - 2 * self.core) % 4
            return jnp.where(
                ahead == 0, 0, jnp.where(ahead == 2, 3, jnp.where(ahead == step, 2, 1))
            )

        return [slot(middle, m) * 4 + slot(ZH, zh) for zh in range(4) for m in range(4)]


def product(left, weight, slots):
    right = jnp.concatenate([weight[slot] for slot in slots], axis=1)
    return lax.dot_general(
        left, right, (((1,), (1,)), ((), ())), preferred_element_type=jnp.float32
    )


def rows_of(width):
    return pl.BlockSpec((ROWS, width), lambda i, place: (i, 0))


def by_core(place):
    return place[0]


def rows_of_own(width, column=lambda place: 0):
    return pl.BlockSpec(
        (ROWS, width), lambda i, place: (jnp.minimum(i, STEPS // 2 - 1), column(place))
    )


def rows_of_other(width, column=lambda place: 0):
    return pl.BlockSpec(
        (ROWS, width), lambda i, place: (jnp.maximum(i - STEPS // 2, 0), column(place))
    )


def whole_weight():
    return pl.BlockSpec((16, PART, LANES), lambda i, place: (0, 0, 0))


def on_own_or_other(own, other, body):
    @pl.when(pl.program_id(0) < STEPS // 2)
    def _():
        body(*own)

    @pl.when(pl.program_id(0) >= STEPS // 2)
    def _():
        body(*other)


def taken(x, layout, arrival, part):
    return jnp.concatenate(
        [x[:, pl.ds(*run)] for run in layout.features(arrival, part)], axis=1
    )


def first_kernel(place, x0, x1, wb, wc, total, last):
    layout = Layout(place)
    depth = 16 * LANES

    def body(x):
        for part, weight in enumerate((wb, wc)):
            columns = slice(part * PART, (part + 1) * PART)
            total[:, columns] = product(
                taken(x, layout, 0, part), weight, layout.slots(part)
            )
            at = part * depth
            for start, width in layout.features(3, part):
                last[:, at : at + width] = x[:, pl.ds(start, width)]
                at += width

    on_own_or_other((x0,), (x1,), body)


def squares_kernel(x, squares):
    sums = jnp.zeros(squares.shape, jnp.float32)
    for k in range(0, x.shape[1], LANES):
        v = x[:, k : k + LANES].astype(jnp.float32)
        sums += v * v
    squares[...] = sums


def sum_squares(x):
    tokens, width = x.shape
    return pl.pallas_call(
        squares_kernel,
        grid=(8,),
        in_specs=[pl.BlockSpec((tokens // 8, width), lambda i: (i, 0))],
        out_specs=pl.BlockSpec((tokens // 8, LANES), lambda i: (i, 0)),
        out_shape=shape((tokens, LANES), jnp.float32),
        compiler_params=params(58),
    )(x)


def estimate(tokens, chunks):
    depth = 16 * LANES
    return pl.CostEstimate(
        flops=4 * tokens * chunks * depth * PART,
        transcendentals=0,
        bytes_accessed=4 * tokens * chunks * depth + 16 * tokens * HALF,
    )


def first(place, x, weights):
    tokens, width = x[0].shape
    depth = 2 * 16 * LANES
    return pl.pallas_call(
        first_kernel,
        grid_spec=pltpu.PrefetchScalarGridSpec(
            num_scalar_prefetch=1,
            grid=(STEPS,),
            in_specs=[rows_of_own(width), rows_of_other(width)] + [whole_weight()] * 2,
            out_specs=[rows_of(HALF), rows_of(depth)],
        ),
        out_shape=[
            shape((2 * tokens, HALF), jnp.float32),
            shape((2 * tokens, depth), jnp.bfloat16),
        ],
        compiler_params=params(34),
        cost_estimate=estimate(tokens, 4),
    )(place, *x, *weights)


def next_kernel(place, x0, x1, wb1, wc1, wb2, wc2, before, total):
    layout = Layout(place)

    def body(x):
        for part, weights in enumerate(((wb1, wb2), (wc1, wc2))):
            columns = slice(part * PART, (part + 1) * PART)
            value = before[:, columns]
            for arrival, weight in enumerate(weights, 1):
                value += product(taken(x, layout, arrival, part), weight, layout.slots(part))
            total[:, columns] = value

    on_own_or_other((x0,), (x1,), body)


def following(place, x, weights, before):
    tokens, width = x[0].shape
    flat = [w for pair in weights for w in pair]
    return pl.pallas_call(
        next_kernel,
        grid_spec=pltpu.PrefetchScalarGridSpec(
            num_scalar_prefetch=1,
            grid=(STEPS,),
            in_specs=[rows_of_own(width), rows_of_other(width)]
            + [whole_weight()] * 4
            + [rows_of(HALF)],
            out_specs=rows_of(HALF),
        ),
        out_shape=shape((2 * tokens, HALF), jnp.float32),
        compiler_params=params(40),
        cost_estimate=estimate(tokens, 4),
    )(place, *x, *flat, before)


def last_kernel(
    place, x, wb, wc, before, squares0, squares1, t0, t1, kv, other_kv, errors, sums
):
    layout = Layout(place)
    step = pl.program_id(0)

    @pl.when(step == 0)
    def _():
        sums[...] = jnp.zeros_like(sums)

    width = 2 * x.shape[1]
    depth = 16 * LANES

    def body(squares, target, out):
        mean = jnp.sum(squares[...], axis=1, keepdims=True) / width
        scale = lax.rsqrt(mean + epsilon)
        for part, weight in enumerate((wb, wc)):
            columns = slice(part * PART, (part + 1) * PART)
            value = product(
                x[:, part * depth : (part + 1) * depth], weight, layout.slots(part)
            )
            exact = (before[:, columns] + value) * scale
            out[:, columns] = exact.astype(jnp.bfloat16)
            error = exact - target[:, columns].astype(jnp.float32)
            error = error * error
            error = error[:, :LANES] + error[:, LANES:]
            sums[...] += jnp.sum(error.reshape(-1, 8, LANES), axis=0)

    on_own_or_other((squares0, t0, kv), (squares1, t1, other_kv), body)

    @pl.when(step == STEPS - 1)
    def _():
        errors[...] = jnp.broadcast_to(jnp.sum(sums[...], axis=0, keepdims=True), errors.shape)


def finish(place, x, weights, before, squares, targets):
    tokens, depth = x.shape[0] // 2, x.shape[1]
    return pl.pallas_call(
        last_kernel,
        grid_spec=pltpu.PrefetchScalarGridSpec(
            num_scalar_prefetch=1,
            grid=(STEPS,),
            in_specs=[rows_of(depth)]
            + [whole_weight()] * 2
            + [rows_of(HALF)]
            + [rows_of_own(LANES), rows_of_other(LANES)]
            + [rows_of_own(HALF, by_core), rows_of_other(HALF, by_core)],
            out_specs=[
                rows_of_own(HALF, by_core),
                rows_of_other(HALF),
                pl.BlockSpec((32, LANES), lambda i, place: (0, 0)),
            ],
            scratch_shapes=[pltpu.VMEM((8, LANES), jnp.float32)],
        ),
        out_shape=[
            shape((tokens, 2 * HALF), jnp.bfloat16),
            shape((tokens, HALF), jnp.bfloat16),
            shape((32, LANES), jnp.float32),
        ],
        compiler_params=params(26),
        cost_estimate=estimate(tokens, 2),
    )(place, x, *weights, before, *squares, *targets)


def swap_rows(everyone, groups):
    return lax.all_to_all(everyone, AXES, 0, 0, axis_index_groups=groups, tiled=True)


def spread_kernel(rows, out):
    out[...] = jnp.broadcast_to(jnp.sum(rows[...], axis=0, keepdims=True), out.shape)


def per_device(
    layer_input_rows,
    input_norm_gain,
    key_value_codes,
    block_scale_codes,
    outer_scale_codes,
    adapter_down_factor,
    adapter_up_factor,
    target,
):
    core = lax.axis_index("grp") % 2
    shard = lax.axis_index("fsdp")

    tokens = layer_input_rows.shape[0]
    other_rows = lax.ppermute(layer_input_rows, AXES, OTHER_CORE)
    place = jnp.stack([core, shard]).astype(jnp.int32)
    other_target = lax.ppermute(target, AXES, OTHER_CORE)

    own_weight = decode(
        key_value_codes,
        block_scale_codes,
        outer_scale_codes,
        input_norm_gain,
        adapter_down_factor,
        adapter_up_factor,
    )
    own_rows, own_weight = lax.optimization_barrier((layer_input_rows, own_weight))
    own_squares = sum_squares(own_rows)
    along_z = ring(own_weight, ZH)
    own_squares, other_target, *along_z = lax.optimization_barrier(
        (own_squares, other_target, *along_z)
    )
    squares = (own_squares, lax.ppermute(own_squares, AXES, OTHER_CORE))
    planes = []
    for part, (middle, last) in enumerate(ORDER):
        columns = slice(part * PART, (part + 1) * PART)
        line = jnp.stack([piece[columns] for piece in along_z])
        planes.append(jnp.concatenate(ring(line, middle)))

    behind = [lax.ppermute(p, AXES, FORWARD[last]) for p, (_, last) in zip(planes, ORDER)]
    ahead = [lax.ppermute(p, AXES, BACKWARD[last]) for p, (_, last) in zip(planes, ORDER)]
    x = (layer_input_rows, other_rows)
    total, last_x = first(place, x, planes)
    total, *behind = lax.optimization_barrier((total, *behind))
    opposite = [lax.ppermute(p, AXES, FORWARD[last]) for p, (_, last) in zip(behind, ORDER)]
    total = following(place, x, [behind, ahead], total)
    kv, other_kv, errors = finish(
        place, last_x, opposite, total, squares, (target, other_target)
    )
    received = lax.ppermute(other_kv, AXES, OTHER_CORE)
    kv = lax.dynamic_update_slice(kv, received, (0, (1 - core) * HALF))

    sums = swap_rows(errors, LOSS_GROUPS[0])
    sums = pl.pallas_call(
        spread_kernel, in_specs=[VMEM], out_specs=VMEM, out_shape=shape((8, LANES), jnp.float32)
    )(sums)
    sums = swap_rows(sums, LOSS_GROUPS[1])
    sums, kv = lax.optimization_barrier((sums, kv))
    loss = jnp.sum(sums) / (tokens * lax.axis_size("fsdp") * 2 * HALF)
    return kv, loss


def solution(mesh):
    placed = (
        P(("grp", "fsdp"), None),
        P(),
        P("fsdp", None),
        P("fsdp", None),
        P("fsdp"),
        P(),
        P(),
        P(("grp", "fsdp"), None),
    )
    return jax.shard_map(
        per_device,
        mesh=mesh,
        in_specs=placed,
        out_specs=(P(("grp", "fsdp"), None), P()),
        check_vma=False,
    )
```

```python
import functools

import numpy as np

import jax
import jax.numpy as jnp
from jax import lax
from jax.experimental import pallas as pl
from jax.experimental.pallas import tpu as pltpu
from jax.sharding import PartitionSpec as P

adapter_scale = 0.25
epsilon = 1e-06
nf4_levels = (
    -1.0,
    -0.6961928009986877,
    -0.5250730514526367,
    -0.39491748809814453,
    -0.28444138169288635,
    -0.18477343022823334,
    -0.09105003625154495,
    0.0,
    0.07958029955625534,
    0.16093020141124725,
    0.24611230194568634,
    0.33791524171066284,
    0.44070982933044434,
    0.5626170039176941,
    0.7229568362236023,
    1.0,
)

AXES = ("grp", "fsdp")
LANES = 128
PART = 256
HALF = 2 * PART


def permutation(move):
    sizes = (2, 2, 4, 4, 4)
    pairs = []
    for source in range(int(np.prod(sizes))):
        place = [int(v) for v in np.unravel_index(source, sizes)]
        target = [v % s for v, s in zip(move(*place), sizes)]
        pairs.append((source, int(np.ravel_multi_index(target, sizes))))
    return pairs


def along(axis, step):
    def move(*place):
        place = list(place)
        place[axis] += step if place[1] == 0 else -step
        return place

    return permutation(move)


ZH, X, Y = 2, 3, 4
FORWARD = {axis: along(axis, 1) for axis in (ZH, X, Y)}
BACKWARD = {axis: along(axis, -1) for axis in (ZH, X, Y)}
ORDER = ((Y, X), (X, Y))
STRIDE = {ZH: 16, X: 4, Y: 1}
ACROSS_ZH = permutation(lambda zl, c, zh, x, y: (1 - zl, c, zh + 2, x, y))
OTHER_CORE = permutation(lambda zl, c, zh, x, y: (zl, 1 - c, zh, x, y))


def ring(block, axis):
    behind = lax.ppermute(block, AXES, FORWARD[axis])
    ahead = lax.ppermute(block, AXES, BACKWARD[axis])
    if axis == ZH:
        opposite = lax.ppermute(block, AXES, ACROSS_ZH)
    else:
        opposite = lax.ppermute(behind, AXES, FORWARD[axis])
    return [block, behind, ahead, opposite]


_DEVICES = np.arange(256).reshape(2, 2, 4, 16).transpose(0, 2, 1, 3).reshape(8, 32)
LOSS_GROUPS = (_DEVICES.tolist(), _DEVICES.T.tolist())


ANY = pl.BlockSpec(memory_space=pl.ANY)
VMEM = pl.BlockSpec(memory_space=pltpu.VMEM)
SMEM = pl.BlockSpec(memory_space=pltpu.SMEM)


def shape(dims, kind):
    return jax.ShapeDtypeStruct(dims, kind)


def params(mib):
    return pltpu.CompilerParams(vmem_limit_bytes=mib << 20)


def decode_kernel(
    outer, words, scale_words, gain, down, up, whole, levels, own_words, own_down, own_up, sems
):
    core = lax.axis_index("grp") % 2
    shard = lax.axis_index("fsdp")
    lanes = pl.ds(pl.multiple_of(core * LANES, LANES), LANES)
    rows = pl.ds(pl.multiple_of(shard * LANES, LANES), LANES)
    half = pl.ds(pl.multiple_of(core * HALF, HALF), HALF)
    copies = [
        pltpu.make_async_copy(words.at[:, lanes], own_words, sems.at[0]),
        pltpu.make_async_copy(down.at[:, rows], own_down, sems.at[1]),
        pltpu.make_async_copy(up.at[:, half], own_up, sems.at[2]),
    ]
    for copy in copies:
        copy.start()
    for copy in copies:
        copy.wait()
    words_t = jnp.transpose(own_words[...])
    for j in range(4):
        code = jnp.bitwise_and(jnp.right_shift(words_t, 4 * j), 15)
        value = jnp.full(code.shape, nf4_levels[0], jnp.float32)
        for number in range(1, 16):
            value = jnp.where(code == number, jnp.float32(nf4_levels[number]), value)
        levels[pl.ds(j, LANES, stride=4), :] = value
    row = lax.broadcasted_iota(jnp.int32, (1, LANES), 1)
    second = jnp.zeros((1, LANES), jnp.float32)
    for g in range(8):
        code = outer[g].astype(jnp.float32)
        second = jnp.where(row // 16 == g, code, second)
    second = jnp.exp2(second / 128.0 - 6.0)
    code_bytes = jnp.concatenate(
        [
            jnp.bitwise_and(jnp.right_shift(scale_words[...], 8 * j), 255).astype(jnp.float32)
            for j in range(4)
        ],
        axis=0,
    ).astype(jnp.bfloat16)
    word_at = lax.broadcasted_iota(jnp.int32, (LANES, LANES), 0)
    row_at = lax.broadcasted_iota(jnp.int32, (LANES, LANES), 1)
    which = lax.broadcasted_iota(jnp.int32, (4, LANES), 0)
    own_rows = which == lax.broadcasted_iota(jnp.int32, (4, LANES), 1) // 32
    adapter = lax.dot_general(
        own_up[...], own_down[...], (((0,), (0,)), ((), ())), preferred_element_type=jnp.float32
    )
    gains = gain[...].astype(jnp.float32).reshape(64, LANES)
    is_own = lax.broadcasted_iota(jnp.int32, gains.shape, 0) == shard
    gain_row = jnp.sum(jnp.where(is_own, gains, 0.0), axis=0, keepdims=True)
    pieces = []
    for q in range(2):
        pick = (word_at == 4 * (row_at % 32) + (2 * core + q)).astype(jnp.float32)
        found = jnp.dot(
            code_bytes, pick.astype(jnp.bfloat16), preferred_element_type=jnp.float32
        )
        for j in range(4):
            code = jnp.sum(
                jnp.where(own_rows, found[4 * j : 4 * j + 4], 0.0), axis=0, keepdims=True
            )
            absmax = (code + 0.5) / 256.0 * second
            block = 4 * q + j
            rows = slice(64 * block, 64 * block + 64)
            weight = levels[rows, :] * absmax + adapter_scale * adapter[rows]
            pieces.append((weight * gain_row).astype(jnp.bfloat16))
    whole[...] = jnp.concatenate(pieces, axis=0)


def decode(words, scale_words, outer, gain, down, up):
    return pl.pallas_call(
        decode_kernel,
        in_specs=[SMEM, ANY, VMEM, VMEM, ANY, ANY],
        out_specs=VMEM,
        out_shape=shape((HALF, LANES), jnp.bfloat16),
        scratch_shapes=[
            pltpu.VMEM((HALF, LANES), jnp.float32),
            pltpu.VMEM((LANES, LANES), jnp.int32),
            pltpu.VMEM((64, LANES), jnp.bfloat16),
            pltpu.VMEM((64, HALF), jnp.bfloat16),
            pltpu.SemaphoreType.DMA((3,)),
        ],
    )(outer, words, scale_words, gain, down.T, up)


def ring_offset(core, j):
    step = 1 - 2 * core
    return jnp.where(j == 0, 0, jnp.where(j == 1, -step, jnp.where(j == 2, step, 2)))


ROWS = 256
STEPS = 4


class Layout:
    def __init__(self, place):
        self.core, own = place[0], place[1]
        self.position = {ZH: own // 16, X: (own // 4) % 4, Y: own % 4}

    def features(self, arrival, part):
        middle, last = ORDER[part]
        at = (self.position[last] + ring_offset(self.core, arrival)) % 4 * STRIDE[last]
        width = 4 if middle == Y else 1
        for spot in range(0, 16, width):
            shard = spot // 4 * 16 + spot % 4 * STRIDE[middle] + at
            yield pl.multiple_of(shard * LANES, width * LANES), width * LANES

    def slots(self, part):
        middle, _ = ORDER[part]

        def slot(axis, place):
            ahead = (place - self.position[axis]) % 4
            step = (1 - 2 * self.core) % 4
            return jnp.where(
                ahead == 0, 0, jnp.where(ahead == 2, 3, jnp.where(ahead == step, 2, 1))
            )

        return [slot(middle, m) * 4 + slot(ZH, zh) for zh in range(4) for m in range(4)]


def product(left, weight, slots):
    right = jnp.concatenate([weight[slot] for slot in slots], axis=1)
    return lax.dot_general(
        left, right, (((1,), (1,)), ((), ())), preferred_element_type=jnp.float32
    )


def rows_of(width):
    return pl.BlockSpec((ROWS, width), lambda i, place: (i, 0))


def by_core(place):
    return place[0]


def rows_of_own(width, column=lambda place: 0):
    return pl.BlockSpec(
        (ROWS, width), lambda i, place: (jnp.minimum(i, STEPS // 2 - 1), column(place))
    )


def rows_of_other(width, column=lambda place: 0):
    return pl.BlockSpec(
        (ROWS, width), lambda i, place: (jnp.maximum(i - STEPS // 2, 0), column(place))
    )


def whole_weight():
    return pl.BlockSpec((16, PART, LANES), lambda i, place: (0, 0, 0))


def on_own_or_other(own, other, body):
    @pl.when(pl.program_id(0) < STEPS // 2)
    def _():
        body(*own)

    @pl.when(pl.program_id(0) >= STEPS // 2)
    def _():
        body(*other)


def taken(x, layout, arrival, part):
    return jnp.concatenate(
        [x[:, pl.ds(*run)] for run in layout.features(arrival, part)], axis=1
    )


def first_kernel(place, x0, x1, wb, wc, total, last):
    layout = Layout(place)
    depth = 16 * LANES

    def body(x):
        for part, weight in enumerate((wb, wc)):
            columns = slice(part * PART, (part + 1) * PART)
            total[:, columns] = product(
                taken(x, layout, 0, part), weight, layout.slots(part)
            )
            at = part * depth
            for start, width in layout.features(3, part):
                last[:, at : at + width] = x[:, pl.ds(start, width)]
                at += width

    on_own_or_other((x0,), (x1,), body)


def squares_kernel(x, squares):
    sums = jnp.zeros(squares.shape, jnp.float32)
    for k in range(0, x.shape[1], LANES):
        v = x[:, k : k + LANES].astype(jnp.float32)
        sums += v * v
    squares[...] = sums


def sum_squares(x):
    tokens, width = x.shape
    return pl.pallas_call(
        squares_kernel,
        grid=(8,),
        in_specs=[pl.BlockSpec((tokens // 8, width), lambda i: (i, 0))],
        out_specs=pl.BlockSpec((tokens // 8, LANES), lambda i: (i, 0)),
        out_shape=shape((tokens, LANES), jnp.float32),
        compiler_params=params(58),
    )(x)


def estimate(tokens, chunks):
    depth = 16 * LANES
    return pl.CostEstimate(
        flops=4 * tokens * chunks * depth * PART,
        transcendentals=0,
        bytes_accessed=4 * tokens * chunks * depth + 16 * tokens * HALF,
    )


def first(place, x, weights):
    tokens, width = x[0].shape
    depth = 2 * 16 * LANES
    return pl.pallas_call(
        first_kernel,
        grid_spec=pltpu.PrefetchScalarGridSpec(
            num_scalar_prefetch=1,
            grid=(STEPS,),
            in_specs=[rows_of_own(width), rows_of_other(width)] + [whole_weight()] * 2,
            out_specs=[rows_of(HALF), rows_of(depth)],
        ),
        out_shape=[
            shape((2 * tokens, HALF), jnp.float32),
            shape((2 * tokens, depth), jnp.bfloat16),
        ],
        compiler_params=params(34),
        cost_estimate=estimate(tokens, 4),
    )(place, *x, *weights)


def next_kernel(place, x0, x1, wb1, wc1, wb2, wc2, before, total):
    layout = Layout(place)

    def body(x):
        for part, weights in enumerate(((wb1, wb2), (wc1, wc2))):
            columns = slice(part * PART, (part + 1) * PART)
            value = before[:, columns]
            for arrival, weight in enumerate(weights, 1):
                value += product(taken(x, layout, arrival, part), weight, layout.slots(part))
            total[:, columns] = value

    on_own_or_other((x0,), (x1,), body)


def following(place, x, weights, before):
    tokens, width = x[0].shape
    flat = [w for pair in weights for w in pair]
    return pl.pallas_call(
        next_kernel,
        grid_spec=pltpu.PrefetchScalarGridSpec(
            num_scalar_prefetch=1,
            grid=(STEPS,),
            in_specs=[rows_of_own(width), rows_of_other(width)]
            + [whole_weight()] * 4
            + [rows_of(HALF)],
            out_specs=rows_of(HALF),
        ),
        out_shape=shape((2 * tokens, HALF), jnp.float32),
        compiler_params=params(40),
        cost_estimate=estimate(tokens, 4),
    )(place, *x, *flat, before)


def last_kernel(
    place, x, wb, wc, before, squares0, squares1, t0, t1, kv, other_kv, errors, sums
):
    layout = Layout(place)
    step = pl.program_id(0)

    @pl.when(step == 0)
    def _():
        sums[...] = jnp.zeros_like(sums)

    width = 2 * x.shape[1]
    depth = 16 * LANES

    def body(squares, target, out):
        mean = jnp.sum(squares[...], axis=1, keepdims=True) / width
        scale = lax.rsqrt(mean + epsilon)
        for part, weight in enumerate((wb, wc)):
            columns = slice(part * PART, (part + 1) * PART)
            value = product(
                x[:, part * depth : (part + 1) * depth], weight, layout.slots(part)
            )
            exact = (before[:, columns] + value) * scale
            out[:, columns] = exact.astype(jnp.bfloat16)
            error = exact - target[:, columns].astype(jnp.float32)
            error = error * error
            error = error[:, :LANES] + error[:, LANES:]
            sums[...] += jnp.sum(error.reshape(-1, 8, LANES), axis=0)

    on_own_or_other((squares0, t0, kv), (squares1, t1, other_kv), body)

    @pl.when(step == STEPS - 1)
    def _():
        errors[...] = jnp.broadcast_to(jnp.sum(sums[...], axis=0, keepdims=True), errors.shape)


def finish(place, x, weights, before, squares, targets):
    tokens, depth = x.shape[0] // 2, x.shape[1]
    return pl.pallas_call(
        last_kernel,
        grid_spec=pltpu.PrefetchScalarGridSpec(
            num_scalar_prefetch=1,
            grid=(STEPS,),
            in_specs=[rows_of(depth)]
            + [whole_weight()] * 2
            + [rows_of(HALF)]
            + [rows_of_own(LANES), rows_of_other(LANES)]
            + [rows_of_own(HALF, by_core), rows_of_other(HALF, by_core)],
            out_specs=[
                rows_of_own(HALF, by_core),
                rows_of_other(HALF),
                pl.BlockSpec((32, LANES), lambda i, place: (0, 0)),
            ],
            scratch_shapes=[pltpu.VMEM((8, LANES), jnp.float32)],
        ),
        out_shape=[
            shape((tokens, 2 * HALF), jnp.bfloat16),
            shape((tokens, HALF), jnp.bfloat16),
            shape((32, LANES), jnp.float32),
        ],
        compiler_params=params(26),
        cost_estimate=estimate(tokens, 2),
    )(place, x, *weights, before, *squares, *targets)


def swap_rows(everyone, groups):
    return lax.all_to_all(everyone, AXES, 0, 0, axis_index_groups=groups, tiled=True)


def spread_kernel(rows, out):
    out[...] = jnp.broadcast_to(jnp.sum(rows[...], axis=0, keepdims=True), out.shape)


def per_device(
    layer_input_rows,
    input_norm_gain,
    key_value_codes,
    block_scale_codes,
    outer_scale_codes,
    adapter_down_factor,
    adapter_up_factor,
    target,
):
    core = lax.axis_index("grp") % 2
    shard = lax.axis_index("fsdp")

    tokens = layer_input_rows.shape[0]
    other_rows = lax.ppermute(layer_input_rows, AXES, OTHER_CORE)
    place = jnp.stack([core, shard]).astype(jnp.int32)
    other_target = lax.ppermute(target, AXES, OTHER_CORE)

    own_weight = decode(
        key_value_codes,
        block_scale_codes,
        outer_scale_codes,
        input_norm_gain,
        adapter_down_factor,
        adapter_up_factor,
    )
    own_rows, own_weight = lax.optimization_barrier((layer_input_rows, own_weight))
    own_squares = sum_squares(own_rows)
    along_z = ring(own_weight, ZH)
    own_squares, *along_z = lax.optimization_barrier((own_squares, *along_z))
    other_squares = lax.ppermute(own_squares, AXES, OTHER_CORE)
    planes = []
    for part, (middle, last) in enumerate(ORDER):
        columns = slice(part * PART, (part + 1) * PART)
        line = jnp.stack([piece[columns] for piece in along_z])
        planes.append(jnp.concatenate(ring(line, middle)))

    behind = [lax.ppermute(p, AXES, FORWARD[last]) for p, (_, last) in zip(planes, ORDER)]
    ahead = [lax.ppermute(p, AXES, BACKWARD[last]) for p, (_, last) in zip(planes, ORDER)]
    own_rows, other_squares = lax.optimization_barrier((layer_input_rows, other_squares))
    squares = (own_squares, other_squares)
    x = (own_rows, other_rows)
    total, last_x = first(place, x, planes)
    total, *behind = lax.optimization_barrier((total, *behind))
    opposite = [lax.ppermute(p, AXES, FORWARD[last]) for p, (_, last) in zip(behind, ORDER)]
    total = following(place, x, [behind, ahead], total)
    kv, other_kv, errors = finish(
        place, last_x, opposite, total, squares, (target, other_target)
    )
    received = lax.ppermute(other_kv, AXES, OTHER_CORE)
    kv = lax.dynamic_update_slice(kv, received, (0, (1 - core) * HALF))

    sums = swap_rows(errors, LOSS_GROUPS[0])
    sums = pl.pallas_call(
        spread_kernel, in_specs=[VMEM], out_specs=VMEM, out_shape=shape((8, LANES), jnp.float32)
    )(sums)
    sums = swap_rows(sums, LOSS_GROUPS[1])
    sums, kv = lax.optimization_barrier((sums, kv))
    loss = jnp.sum(sums) / (tokens * lax.axis_size("fsdp") * 2 * HALF)
    return kv, loss


def solution(mesh):
    placed = (
        P(("grp", "fsdp"), None),
        P(),
        P("fsdp", None),
        P("fsdp", None),
        P("fsdp"),
        P(),
        P(),
        P(("grp", "fsdp"), None),
    )
    return jax.shard_map(
        per_device,
        mesh=mesh,
        in_specs=placed,
        out_specs=(P(("grp", "fsdp"), None), P()),
        check_vma=False,
    )
```
